512 devices in a mesh: seq: 128 (over y, z, core), tp: 4 (over x).
Axes of the slice: x: 4, y: 8, z: 8, core: 2. Of those that a mesh axis runs over, the one named last changes fastest.
Arguments:
- features: bfloat16 [16384, 3, 4096], P('seq', None, 'tp'), may hold values from -6 to 6
- short_taps: bfloat16 [3, 3, 4096], P(None, None, 'tp'), may hold values from -3.5 to 3.5
- rates: float32 [4096, 16], P('tp'), may hold values from 6.1035156e-06 to 0.2
- residues: float32 [4096, 16], P('tp'), may hold values from -0.0625 to 0.0625
- skip: float32 [4096], P('tp'), may hold values from -6 to 6
- out_weight: bfloat16 [4096, 4096], P('seq', 'tp'), may hold values from -0.09375 to 0.09375
Outputs:
- layer_out: bfloat16 [16384, 4096], P('seq', 'tp')
The draws below stay inside these ranges and needn't reach their ends.
All inputs are finite; a program needn't handle non-finite values.
Results may differ from the reference program's by a relative error of at most 0.025.
Values may be sent and summed in bfloat16 or wider, within the bound.
A program may use at most 128 MiB of HBM per device.

```python
import math
import jax
import jax.numpy as jnp
from jax import lax

D = 4096
R = 16
SHORT = 3
TOK_DEV = 128
TOKENS = 16384
N_TP = 4


def draw_rates(key, part):
    key_slow, key_fast, key_pick = jax.random.split(key, 3)
    slow_rates = jnp.exp(jax.random.uniform(key_slow, (D, R), jnp.float32, math.log(0.1 / TOKENS), math.log(2.0 / TOKENS)))
    fast_rates = jnp.exp(jax.random.uniform(key_fast, (D, R), jnp.float32, math.log(0.04), math.log(0.2)))
    share = 0.5
    picked = jax.random.uniform(key_pick, (D, R), jnp.float32) < share
    return jnp.where(picked, slow_rates, fast_rates).astype(jnp.float32)


def levels(rng, extent, cuts, least, top_value):
    def one(axis_at, shards_of):
        draws = jax.random.uniform(jax.random.fold_in(jax.random.fold_in(rng, 6), axis_at), (shards_of,), jnp.float32, least / len(cuts), top_value / len(cuts))
        return jnp.repeat(jnp.exp(draws), extent[axis_at] // shards_of).reshape((-1,) + (1,) * (len(extent) - axis_at - 1))

    level = one(*cuts[0])
    for cut in cuts[1:]:
        level = level * one(*cut)
    return level


def normal_values(stream_key, dims, width, limit, pieces=(), held_as=jnp.bfloat16):
    drawn = width * jax.random.normal(stream_key, dims, jnp.float32)
    if pieces:
        drawn = drawn * levels(stream_key, dims, pieces, -0.22, 0.18)
    return jnp.clip(drawn, -limit, limit).astype(held_as)


def setup_inputs(seed: int = 0) -> dict:
    keys = jax.random.split(jax.random.key(seed), 7)
    return {
        "features": normal_values(keys[0], (TOKENS, 3, D), 1.0, 6.0, ((0, 128), (2, 4))),
        "short_taps": normal_values(keys[1], (3, SHORT, D), SHORT ** -0.5, 3.5, ((2, 4),)),
        "rates": draw_rates(jax.random.fold_in(keys[6], 71), 0),
        "residues": normal_values(keys[3], (D, R), (2.0 * (R * TOKENS) ** -0.5), 0.0625, ((0, 4),), jnp.float32),
        "skip": normal_values(keys[4], (D,), 1.0, 6.0, ((0, 4),), jnp.float32),
        "out_weight": normal_values(keys[5], (D, D), D ** -0.5, 0.09375, ((0, 128), (1, 4))),
    }


def short_mix(features, short_taps):
    signal = features.astype(jnp.float32)
    tap_values = short_taps.astype(jnp.float32)
    mixed = tap_values[:, 0, :] * signal
    for shift_rows in range(1, SHORT):
        moved = jnp.concatenate([jnp.zeros((shift_rows,) + signal.shape[1:], jnp.float32), signal[:-shift_rows]], axis=0)
        mixed = mixed + tap_values[:, shift_rows, :] * moved
    return mixed


def reference(features, short_taps, rates, residues, skip, out_weight):
    mixed = short_mix(features, short_taps)
    signal = mixed[:, 1, :] * mixed[:, 2, :]
    step_decay = jnp.exp(-rates)
    block_decay = jnp.exp(-rates * TOK_DEV)
    offsets = jnp.arange(1, TOK_DEV + 1).astype(jnp.float32)
    far_weight = residues[None] * jnp.exp(-rates[None] * offsets[:, None, None])

    def advance(modes, current):
        modes = step_decay * modes + current[:, None]
        return modes, jnp.sum(residues * modes, axis=1)

    def per_block(state, block_signal):
        block_end, near_part = lax.scan(advance, jnp.zeros((D, R), jnp.float32), block_signal)
        far_part = jnp.sum(far_weight * state[None], axis=2)
        return block_decay * state + block_end, near_part + far_part

    _, filtered = lax.scan(per_block, jnp.zeros((D, R), jnp.float32), signal.reshape(TOKENS // TOK_DEV, TOK_DEV, D))
    conv = filtered.reshape(TOKENS, D) + skip[None] * signal
    gated = (mixed[:, 0, :] * conv).astype(jnp.bfloat16)
    group = D // N_TP
    total = jnp.zeros((TOKENS, D), jnp.float32)
    for index in range(N_TP):
        lower = index * group
        part_sum = jnp.dot(gated[:, lower:lower + group], out_weight[:, lower:lower + group].T, preferred_element_type=jnp.float32)
        part_sum = lax.optimization_barrier(part_sum.astype(jnp.bfloat16)).astype(jnp.float32)
        total = total + part_sum
    return total.astype(jnp.bfloat16)
```

```python
import jax
import jax.numpy as jnp
from jax import lax
from jax.experimental import pallas as pl
from jax.experimental.pallas import tpu as pltpu
from jax.sharding import PartitionSpec as P

MESH = pl.DeviceIdType.MESH
F32, BF16 = jnp.float32, jnp.bfloat16
N = 8
TOK, CH, POLES, OUTS = 128, 1024, 16, 4096
BLK, STEPS = 8, 16
LANES = CH // 128
HALF = CH // 2
DIRS = (1, -1)


class Copies:
    def __init__(self, send_sem, recv_sem):
        self.send_sem, self.recv_sem, self.used, self.sent = send_sem, recv_sem, 0, []

    def ids(self, count):
        first = self.used
        self.used += count
        return first

    def make(self, index, src, dst, device):
        return pltpu.make_async_remote_copy(
            src_ref=src,
            dst_ref=dst,
            send_sem=self.send_sem.at[index],
            recv_sem=self.recv_sem.at[index],
            device_id=device,
            device_id_type=MESH,
        )

    def send(self, index, src, dst, device):
        copy = self.make(index, src, dst, device)
        copy.start()
        self.sent.append(copy)


def kernel(
    feat_hbm, taps_ref, rate_ref, res_ref, skip_ref, w_hbm, out_ref,
    wbuf, featb, halo, x, u, m0, taps, dec, ent, ends, ends_b, sib_ends,
    chip_end, y_in, col_b, colp_b, z_in, col, enter, enter_b, sib_enter,
    g, gb, own, part, diag, arrived, send_sem, recv_sem, local_sem,
):
    s, t = lax.axis_index("seq"), lax.axis_index("tp")
    c, q = lax.rem(s, 2), lax.div(s, 2)
    z, y = lax.rem(q, N), lax.div(q, N)
    copies = Copies(send_sem, recv_sem)

    def at(y_of, z_of, c_of):
        return ((y_of * N + z_of) * 2 + c_of, t)

    def ring(i, by):
        return lax.rem(i + by + N, N)

    sib = at(y, z, 1 - c)
    after, before = lax.rem(s + 1, 2 * N * N), lax.rem(s + 2 * N * N - 1, 2 * N * N)
    x_next, x_prev, x_far = lax.rem(t + 1, 4), lax.rem(t + 3, 4), lax.rem(t + 2, 4)

    load_w = [
        pltpu.make_async_copy(w_hbm.at[pl.ds(16 * p, 16)], wbuf.at[y, z, c, p], local_sem.at[p])
        for p in range(2)
    ]
    load_f = pltpu.make_async_copy(feat_hbm, featb, local_sem.at[2])
    for copy in load_w:
        copy.start()
    load_f.start()
    barrier = pltpu.get_barrier_semaphore()
    far_seq = jnp.where(c == 0, before, after)
    partners = [sib, (far_seq, t), (s, x_next), (s, x_prev)]
    for by in DIRS:
        partners += [at(y, ring(z, by), c), at(ring(y, by), z, c)]
    for partner in partners:
        pl.semaphore_signal(barrier, inc=1, device_id=partner, device_id_type=MESH)
    pl.semaphore_wait(barrier, len(partners))

    streams = [(p, d) for d in (0, 1) for p in (0, 1)]
    ring1 = {st: copies.ids(4) for st in streams}
    ring2 = {st: copies.ids(8) for st in streams}
    fwd2 = {st: copies.ids(8) for st in streams}
    fwd1 = {p: copies.ids(1) for p in (0, 1)}

    def lanes(half):
        return pl.ds(0, CH) if half is None else pl.ds(half * HALF, HALF)

    def target(p, d, first):
        along_z = (p == 0) == first
        return at(y, ring(z, DIRS[d]), c) if along_z else at(ring(y, DIRS[d]), z, c)

    def piece1(p, origin, half):
        if p == 0:
            return wbuf.at[y, origin, c, 0, :, lanes(half)]
        return wbuf.at[origin, z, c, 1, :, lanes(half)]

    def piece2(p, origin, half, core):
        if p == 0:
            return wbuf.at[origin, :, core, 0, :, lanes(half)]
        return wbuf.at[:, origin, core, 1, :, lanes(half)]

    def home(p, first):
        return z if (p == 0) == first else y

    def send1(st, k):
        p, d = st
        ref = piece1(p, ring(home(p, True), -DIRS[d] * k), d if k == 3 else None)
        copies.send(ring1[st] + k, ref, ref, target(p, d, True))

    def recv1(st, k):
        p, d = st
        ref = piece1(p, ring(home(p, True), -DIRS[d] * (k + 1)), d if k == 3 else None)
        copies.make(ring1[st] + k, ref, ref, sib).wait_recv()

    def send2(st, k, h):
        p, d = st
        ref = piece2(p, ring(home(p, False), -DIRS[d] * k), h, c)
        copies.send(ring2[st] + 2 * k + h, ref, ref, target(p, d, False))

    def recv2(st, k, h):
        p, d = st
        ref = piece2(p, ring(home(p, False), -DIRS[d] * (k + 1)), h, c)
        copies.make(ring2[st] + 2 * k + h, ref, ref, sib).wait_recv()

    def forward2(st, k, h):
        p, d = st
        ref = piece2(p, ring(home(p, False), -DIRS[d] * (k + 1)), h, c)
        copies.send(fwd2[st] + 2 * k + h, ref, ref, sib)

    def forwarded2(st, k, h):
        p, d = st
        ref = piece2(p, ring(home(p, False), -DIRS[d] * (k + 1)), h, 1 - c)
        copies.make(fwd2[st] + 2 * k + h, ref, ref, sib).wait_recv()

    def phase1(k):
        for st in streams:
            recv1(st, k)
            if k < 3:
                send1(st, k + 1)

    def phase2(k, h):
        for st in streams:
            if k == 3 and h != st[1]:
                continue
            recv2(st, k, h)
            if k < 2 or (k == 2 and h == st[1]):
                send2(st, k + 1, h)
            forward2(st, k, h)

    for copy in load_w:
        copy.wait()
    for st in streams:
        send1(st, 0)
    halo_id = copies.ids(1)
    copies.send(halo_id, feat_hbm.at[:, pl.ds(TOK - 8, 8), :], halo, (after, t))

    taps[...] = taps_ref[...].astype(F32)
    rate = rate_ref[...]
    for k, span in enumerate((1, 16, 32, 64, 128)):
        dec[k] = jnp.exp(-rate * float(span))
    load_f.wait()
    for group in range(3):
        for lane in range(LANES):
            cut = slice(lane * 128, (lane + 1) * 128)
            x[group, lane, pl.ds(8, TOK), :] = featb[group, :, cut].astype(F32)
    phase1(0)
    copies.make(halo_id, halo, halo, sib).wait_recv()
    for group in range(3):
        for lane in range(LANES):
            cut = slice(lane * 128, (lane + 1) * 128)
            edge = jnp.where(s > 0, halo[group, :, cut].astype(F32), 0.0)
            x[group, lane, pl.ds(0, 8), :] = edge

    def row(ref, *index):
        return jnp.broadcast_to(ref[index], (BLK, 128))

    def mix(lane, carry):
        col_at = pl.ds(pl.multiple_of(lane * 128, 128), 128)

        def mixed(group):
            w = [row(taps, group, pl.ds(k, 1), col_at) for k in range(3)]
            v = [x[group, lane, pl.ds(6 + i, BLK, stride=STEPS), :] for i in range(STEPS + 2)]
            return [w[0] * v[i + 2] + w[1] * v[i + 1] + w[2] * v[i] for i in range(STEPS)]

        one, two = mixed(1), mixed(2)
        for i in range(STEPS):
            u[i, :, col_at] = one[i] * two[i]
        for i, value in enumerate(mixed(0)):
            m0[i, :, col_at] = value
        return carry

    lax.fori_loop(0, LANES, mix, 0)
    phase1(1)

    block = lax.broadcasted_iota(jnp.int32, (BLK, 128), 0)

    def shifted(value, by):
        return jnp.where(block >= by, pltpu.roll(value, by, axis=0), 0.0)

    def pass1(lane, carry):
        col_at = pl.ds(pl.multiple_of(lane * 128, 128), 128)
        values = [u[i, :, col_at] for i in range(STEPS)]
        for pole in range(POLES):
            step = row(dec, 0, pl.ds(pole, 1), col_at)
            state = values[0]
            for i in range(1, STEPS):
                state = step * state + values[i]
            for k, by in ((1, 1), (2, 2), (3, 4)):
                state = state + row(dec, k, pl.ds(pole, 1), col_at) * shifted(state, by)
            ent[pole, :, col_at] = shifted(state, 1)
            ends[pl.ds(pole, 1), col_at] = state[BLK - 1 :, :]
        return carry

    lax.fori_loop(0, LANES, pass1, 0)
    ends_b[...] = ends[...].astype(BF16)
    sib_id = copies.ids(1)
    copies.send(sib_id, ends_b, sib_ends, sib)
    phase1(2)

    mine = pl.ds(pl.multiple_of(c * HALF, HALF), HALF)
    rate_h = rate_ref[:, mine]

    def decay(tokens):
        return jnp.exp(-rate_h * float(tokens))

    copies.make(sib_id, sib_ends, sib_ends, sib).wait_recv()
    own_end, other_end = ends[:, mine], sib_ends[:, mine].astype(F32)
    first_end = jnp.where(c == 0, own_end, other_end)
    second_end = jnp.where(c == 0, other_end, own_end)
    total = decay(128) * first_end + second_end
    chip_end[...] = total.astype(BF16)
    phase1(3)

    y_id, z_id, zw_id = copies.ids(N), copies.ids(N), copies.ids(1)
    for k in range(1, N):

        @pl.when(y + k < N)
        def _(k=k):
            copies.make(y_id + k, chip_end, y_in.at[k], at(y + k, z, c)).start()

    for h in (0, 1):
        for st in streams:
            send2(st, 0, h)
    for p in (0, 1):
        ref = piece2(p, home(p, False), None, c)
        copies.send(fwd1[p], ref, ref, sib)

    col[...] = jnp.zeros_like(col)
    for k in range(1, N):

        @pl.when(y >= k)
        def _(k=k):
            copies.make(y_id + k, y_in.at[k], y_in.at[k], sib).wait_recv()
            col[...] += decay(2048 * (k - 1)) * y_in[k].astype(F32)

    col_b[...] = col[...].astype(BF16)
    colp_b[...] = (total + decay(2048) * col[...]).astype(BF16)
    for k in range(1, N):

        @pl.when(z + k < N)
        def _(k=k):
            copies.make(z_id + k, colp_b, z_in.at[k], at(y, z + k, c)).start()

        @pl.when(z + k >= N)
        def _(k=k):
            copies.make(z_id + k, col_b, z_in.at[k], at(y, z + k - N, c)).start()

    phase2(0, 0)
    phase2(0, 1)

    state = decay(256 * 7) * col[...]
    for k in range(1, N):
        copies.make(z_id + k, z_in.at[k], z_in.at[k], sib).wait_recv()
        state = state + decay(256 * (k - 1)) * z_in[k].astype(F32)
    enter_b[...] = state.astype(BF16)
    enter[:, mine] = state
    enter_id = copies.ids(1)
    copies.send(enter_id, enter_b, sib_enter, sib)
    phase2(1, 0)
    copies.make(enter_id, sib_enter, sib_enter, sib).wait_recv()
    theirs = pl.ds(pl.multiple_of((1 - c) * HALF, HALF), HALF)
    enter[:, theirs] = sib_enter[...].astype(F32)

    @pl.when(c == 1)
    def _():
        enter[...] = dec[4] * enter[...] + sib_ends[...].astype(F32)

    phase2(1, 1)

    far = (-float(STEPS)) * block.astype(F32)

    def pass2(lane, carry):
        col_at = pl.ds(pl.multiple_of(lane * 128, 128), 128)
        values = [u[i, :, col_at] for i in range(STEPS)]
        skip = row(skip_ref, pl.ds(0, 1), col_at)

        def one_pole(pole, sums):
            step = row(dec, 0, pl.ds(pole, 1), col_at)
            gain = row(res_ref, pl.ds(pole, 1), col_at)
            reach = jnp.exp(far * row(rate_ref, pl.ds(pole, 1), col_at))
            state = ent[pole, :, col_at] + reach * row(enter, pl.ds(pole, 1), col_at)
            out = []
            for i in range(STEPS):
                state = step * state + values[i]
                out.append(sums[i] + gain * state)
            return out

        sums = [skip * value for value in values]
        for pole in range(POLES):
            sums = one_pole(pole, sums)
        for i in range(STEPS):
            g[lane, pl.ds(i, BLK, stride=STEPS), :] = m0[i, :, col_at] * sums[i]
        return carry

    lax.fori_loop(0, LANES, pass2, 0)
    for lane in range(LANES):
        gb[:, lane * 128 : (lane + 1) * 128] = g[lane].astype(BF16)

    phase2(2, 0)
    phase2(2, 1)
    phase2(3, 0)
    phase2(3, 1)
    for p in (0, 1):
        ref = piece2(p, home(p, False), None, 1 - c)
        copies.make(fwd1[p], ref, ref, sib).wait_recv()
    for k in range(4):
        for h in (0, 1):
            for st in streams:
                if k < 3 or h == st[1]:
                    forwarded2(st, k, h)

    def project(j, n):
        w = wbuf[2 * j + n // 2, pl.ds(4 * (n % 2), 4)].reshape(256, CH)
        return lax.dot_general(
            gb[...], w, (((1,), (1,)), ((), ())), preferred_element_type=F32
        )

    def chunk(slot, j):
        for n in range(4):
            part[slot, :, n * 256 : (n + 1) * 256] = project(j, n).astype(BF16)

    top, low = pl.ds(0, TOK // 2), pl.ds(TOK // 2, TOK // 2)
    rs = copies.ids(6)
    next_dev, prev_dev = (s, x_next), (s, x_prev)
    chunk(0, x_far)
    copies.send(rs, part.at[0, top], diag.at[0], prev_dev)
    copies.send(rs + 1, part.at[0, low], diag.at[1], next_dev)
    chunk(1, x_next)
    copies.send(rs + 2, part.at[1, top], arrived.at[0, top], next_dev)
    chunk(2, x_prev)
    copies.send(rs + 3, part.at[2, low], arrived.at[1, low], prev_dev)
    copies.make(rs + 1, diag.at[1], diag.at[1], sib).wait_recv()
    part[1, low, :] = (part[1, low, :].astype(F32) + diag[1].astype(F32)).astype(BF16)
    copies.send(rs + 4, part.at[1, low], arrived.at[0, low], next_dev)
    copies.make(rs, diag.at[0], diag.at[0], sib).wait_recv()
    part[2, top, :] = (part[2, top, :].astype(F32) + diag[0].astype(F32)).astype(BF16)
    copies.send(rs + 5, part.at[2, top], arrived.at[1, top], prev_dev)
    for n in range(4):
        own[:, n * 256 : (n + 1) * 256] = project(t, n)
    copies.make(rs + 2, arrived.at[0, top], arrived.at[0, top], sib).wait_recv()
    copies.make(rs + 3, arrived.at[1, low], arrived.at[1, low], sib).wait_recv()
    copies.make(rs + 4, arrived.at[0, low], arrived.at[0, low], sib).wait_recv()
    copies.make(rs + 5, arrived.at[1, top], arrived.at[1, top], sib).wait_recv()
    out_ref[...] = (own[...] + arrived[0].astype(F32) + arrived[1].astype(F32)).astype(BF16)

    for copy in copies.sent:
        copy.wait_send()
    for k in range(1, N):

        @pl.when(y + k < N)
        def _(k=k):
            copies.make(y_id + k, chip_end, y_in.at[k], sib).wait_send()

        copies.make(z_id + k, col_b, z_in.at[k], sib).wait_send()


N_COPIES = 120


def per_device(features, short_taps, rates, residues, skip, out_weight):
    vmem, hbm = pl.BlockSpec(memory_space=pltpu.VMEM), pl.BlockSpec(memory_space=pl.ANY)
    return pl.pallas_call(
        kernel,
        out_shape=jax.ShapeDtypeStruct((TOK, CH), BF16),
        in_specs=[hbm, vmem, vmem, vmem, vmem, hbm],
        out_specs=vmem,
        scratch_shapes=[
            pltpu.VMEM((N, N, 2, 2, 16, CH), BF16),
            pltpu.VMEM((3, TOK, CH), BF16),
            pltpu.VMEM((3, 8, CH), BF16),
            pltpu.VMEM((3, LANES, TOK + 8, 128), F32),
            pltpu.VMEM((STEPS, BLK, CH), F32),
            pltpu.VMEM((STEPS, BLK, CH), F32),
            pltpu.VMEM((3, 3, CH), F32),
            pltpu.VMEM((5, POLES, CH), F32),
            pltpu.VMEM((POLES, BLK, CH), F32),
            pltpu.VMEM((POLES, CH), F32),
            pltpu.VMEM((POLES, CH), BF16),
            pltpu.VMEM((POLES, CH), BF16),
            pltpu.VMEM((POLES, HALF), BF16),
            pltpu.VMEM((N, POLES, HALF), BF16),
            pltpu.VMEM((POLES, HALF), BF16),
            pltpu.VMEM((POLES, HALF), BF16),
            pltpu.VMEM((N, POLES, HALF), BF16),
            pltpu.VMEM((POLES, HALF), F32),
            pltpu.VMEM((POLES, CH), F32),
            pltpu.VMEM((POLES, HALF), BF16),
            pltpu.VMEM((POLES, HALF), BF16),
            pltpu.VMEM((LANES, TOK, 128), F32),
            pltpu.VMEM((TOK, CH), BF16),
            pltpu.VMEM((TOK, CH), F32),
            pltpu.VMEM((3, TOK, CH), BF16),
            pltpu.VMEM((2, TOK // 2, CH), BF16),
            pltpu.VMEM((2, TOK, CH), BF16),
            pltpu.SemaphoreType.DMA((N_COPIES,)),
            pltpu.SemaphoreType.DMA((N_COPIES,)),
            pltpu.SemaphoreType.DMA((3,)),
        ],
        compiler_params=pltpu.CompilerParams(
            collective_id=0, has_side_effects=True, vmem_limit_bytes=48 << 20
        ),
        name="hyena",
    )(
        features.transpose(1, 0, 2),
        short_taps,
        rates.T,
        residues.T,
        skip.reshape(1, CH),
        out_weight,
    )


def solution(mesh):
    in_specs = (
        P("seq", None, "tp"),
        P(None, None, "tp"),
        P("tp", None),
        P("tp", None),
        P("tp"),
        P("seq", "tp"),
    )
    out_specs = P("seq", "tp")
    return jax.shard_map(
        per_device, mesh=mesh, in_specs=in_specs, out_specs=out_specs, check_vma=False
    )
```

```python
import functools

import jax
import jax.numpy as jnp
from jax import lax
from jax.experimental import pallas as pl
from jax.experimental.pallas import tpu as pltpu
from jax.sharding import PartitionSpec as P

MESH = pl.DeviceIdType.MESH
F32, BF16 = jnp.float32, jnp.bfloat16
N = 8
TOK, CH, POLES, OUTS = 128, 1024, 16, 4096
BLK, STEPS = 8, 16
LANES = CH // 128
HALF = CH // 2
DIRS = (1, -1)
POOL = 64
GROUPS = ((0, 1), (1, 3), (3, 5), (5, 7), (7, 8))
OFFSETS = ((0,), (1, -1), (2, -2), (3, -3), (4,))
WIDE = 512


class Copies:
    def __init__(self, send_sem, recv_sem):
        self.send_sem, self.recv_sem, self.used, self.held = send_sem, recv_sem, 0, POOL
        self.pool, self.turn = {}, 0

    def ids(self, count):
        self.used += count
        return self.used - count

    def send_ids(self, count):
        self.held += count
        return self.held - count

    def make(self, index, src, dst, device, held=0):
        return pltpu.make_async_remote_copy(
            src_ref=src,
            dst_ref=dst,
            send_sem=self.send_sem.at[held],
            recv_sem=self.recv_sem.at[index],
            device_id=device,
            device_id_type=MESH,
        )

    def send(self, index, src, dst, device):
        held = self.turn % POOL
        self.turn += 1
        if held in self.pool:
            self.pool[held].wait_send()
        self.pool[held] = self.make(index, src, dst, device, held)
        self.pool[held].start()


def kernel(
    feat_hbm, taps_hbm, rate_hbm, res_hbm, skip_hbm, w_hbm, out_ref,
    wbuf, featb, halo, x, u, m0, taps_ref, rate_ref, res_ref, skip_ref, taps, dec,
    ent, ends, ends_b, sib_ends, chip_end, y_in, col_b, colp_b, z_in, col, enter,
    enter_b, sib_enter, g, gb, own, part, diag, arrived,
    send_sem, recv_sem, local_sem, here_sem,
):
    s, t = lax.axis_index("seq"), lax.axis_index("tp")
    c, q = lax.rem(s, 2), lax.div(s, 2)
    z, y = lax.rem(q, N), lax.div(q, N)
    copies = Copies(send_sem, recv_sem)

    def at(y_of, z_of, c_of):
        return ((y_of * N + z_of) * 2 + c_of, t)

    def ring(i, by):
        return lax.rem(i + by + N, N)

    sib = at(y, z, 1 - c)
    after, before = lax.rem(s + 1, 2 * N * N), lax.rem(s + 2 * N * N - 1, 2 * N * N)
    x_next, x_prev, x_far = lax.rem(t + 1, 4), lax.rem(t + 3, 4), lax.rem(t + 2, 4)

    loads = []

    def load(src, dst):
        copy = pltpu.make_async_copy(src, dst, local_sem.at[len(loads)])
        copy.start()
        loads.append(copy)

    barrier = pltpu.get_barrier_semaphore()
    far_seq = jnp.where(c == 0, before, after)
    around = [(y_z, by) for y_z in (0, 1) for by in DIRS]
    around = [at(ring(y, by), z, c) if y_z else at(y, ring(z, by), c) for y_z, by in around]
    partners = [sib, (far_seq, t), (s, x_next), (s, x_prev)] + around
    for partner in partners:
        pl.semaphore_signal(barrier, inc=1, device_id=partner, device_id_type=MESH)
    for p in range(2):
        load(w_hbm.at[:, pl.ds(HALF * p, HALF)], wbuf.at[p, 0, 0, 0])
    load(feat_hbm, featb)
    load(rate_hbm, rate_ref)
    load(taps_hbm, taps_ref)
    load(res_hbm, res_ref)
    load(skip_hbm, skip_ref)
    pl.semaphore_wait(barrier, len(partners))

    def here(round_of):
        if round_of:
            pl.semaphore_wait(here_sem.at[round_of - 1], len(around))
        if round_of < 3:
            for partner in around:
                pl.semaphore_signal(
                    here_sem.at[round_of], inc=1, device_id=partner, device_id_type=MESH
                )

    streams = [(p, d) for d in (0, 1) for p in (0, 1)]
    last = len(GROUPS) - 1

    def carried(d, k):
        return range(last + 1) if k < 3 else (range(3) if d == 0 else range(3, last + 1))

    ring1 = {st: copies.ids(4) for st in streams}
    ring2 = {
        (st, k, group): copies.ids(1)
        for st in streams for k in range(4) for group in carried(st[1], k)
    }
    over = [copies.ids(2) for _ in GROUPS]

    def slot(d, k):
        return 0 if k == 0 else N - 1 if k == N // 2 else 2 * k - d

    def target(p, d, inner):
        along_z = (p == 0) == inner
        return at(y, ring(z, DIRS[d]), c) if along_z else at(ring(y, DIRS[d]), z, c)

    def send1(p, d, k):
        src, dst = wbuf.at[p, 0, 0, slot(d, k)], wbuf.at[p, 0, 0, slot(d, k + 1)]
        copies.send(ring1[p, d] + k, src, dst, target(p, d, True))

    def recv1(p, d, k):
        ref = wbuf.at[p, 0, 0, slot(d, k + 1)]
        copies.make(ring1[p, d] + k, ref, ref, sib).wait_recv()

    def outer(p, d, k, group, core=0):
        low, high = GROUPS[group]
        return wbuf.at[p, core, slot(d, k), low:high]

    def send2(p, d, k, group):
        src, dst = outer(p, d, k, group), outer(p, d, k + 1, group)
        copies.send(ring2[(p, d), k, group], src, dst, target(p, d, False))

    def recv2(p, d, k, group):
        ref = outer(p, d, k + 1, group)
        copies.make(ring2[(p, d), k, group], ref, ref, sib).wait_recv()

    def over_refs(m, core):
        low, high = GROUPS[m]
        return wbuf.at[0, core, low:high], wbuf.at[1, core, :, low:high]

    def stage(n):
        if 1 <= n <= 4:
            for p, d in streams:
                if n < 4 or d == 1:
                    recv1(p, d, n - 1)
                if n < 3 or (n == 3 and d == 1):
                    send1(p, d, n)
        if n == 0:
            for p, d in streams:
                send1(p, d, 0)
        if n <= last:
            for p, d in streams:
                send2(p, d, 0, n)
        for k in range(4):
            group = n - 1 - k
            if not 0 <= group <= last:
                continue
            for p, d in streams:
                if group not in carried(d, k):
                    continue
                recv2(p, d, k, group)
                if k < 3 and group in carried(d, k + 1):
                    send2(p, d, k + 1, group)
        if n >= 4:
            for p in (0, 1):
                src, dst = over_refs(n - 4, 0)[p], over_refs(n - 4, 1)[p]
                copies.send(over[n - 4] + p, src, dst, sib)

    def gathered(m):
        for p in (0, 1):
            ref = over_refs(m, 1)[p]
            copies.make(over[m] + p, ref, ref, sib).wait_recv()

    halo_id = copies.ids(1)
    copies.send(halo_id, feat_hbm.at[:, pl.ds(TOK - 8, 8), :], halo, (after, t))
    here(0)
    for copy in loads[:2]:
        copy.wait()
    stage(0)

    for copy in loads[2:]:
        copy.wait()
    taps[...] = taps_ref[...].astype(F32)
    rate = rate_ref[...]
    for k, span in enumerate((1, 16, 32, 64, 128)):
        dec[k] = jnp.exp(-rate * float(span))
    for group in range(3):
        for lane in range(LANES):
            cut = slice(lane * 128, (lane + 1) * 128)
            x[group, lane, pl.ds(8, TOK), :] = featb[group, :, cut].astype(F32)
    stage(1)
    here(1)
    copies.make(halo_id, halo, halo, sib).wait_recv()
    for group in range(3):
        for lane in range(LANES):
            cut = slice(lane * 128, (lane + 1) * 128)
            edge = jnp.where(s > 0, halo[group, :, cut].astype(F32), 0.0)
            x[group, lane, pl.ds(0, 8), :] = edge

    def row(ref, *index):
        return jnp.broadcast_to(ref[index], (BLK, 128))

    def mix(lane, carry):
        col_at = pl.ds(pl.multiple_of(lane * 128, 128), 128)

        def mixed(group):
            w = [row(taps, group, pl.ds(k, 1), col_at) for k in range(3)]
            v = [x[group, lane, pl.ds(6 + i, BLK, stride=STEPS), :] for i in range(STEPS + 2)]
            return [w[0] * v[i + 2] + w[1] * v[i + 1] + w[2] * v[i] for i in range(STEPS)]

        one, two = mixed(1), mixed(2)
        for i in range(STEPS):
            u[i, :, col_at] = one[i] * two[i]
        for i, value in enumerate(mixed(0)):
            m0[i, :, col_at] = value
        return carry

    lax.fori_loop(0, LANES, mix, 0)

    block = lax.broadcasted_iota(jnp.int32, (BLK, 128), 0)

    def shifted(value, by):
        return jnp.where(block >= by, pltpu.roll(value, by, axis=0), 0.0)

    def pass1(lane, carry):
        col_at = pl.ds(pl.multiple_of(lane * 128, 128), 128)
        values = [u[i, :, col_at] for i in range(STEPS)]
        for pole in range(POLES):
            fade = row(dec, 0, pl.ds(pole, 1), col_at)
            state = values[0]
            for i in range(1, STEPS):
                state = fade * state + values[i]
            for k, by in ((1, 1), (2, 2), (3, 4)):
                state = state + row(dec, k, pl.ds(pole, 1), col_at) * shifted(state, by)
            ent[pole, :, col_at] = shifted(state, 1)
            ends[pl.ds(pole, 1), col_at] = state[BLK - 1 :, :]
        return carry

    lax.fori_loop(0, LANES, pass1, 0)
    ends_b[...] = ends[...].astype(BF16)
    sib_id = copies.ids(1)
    copies.send(sib_id, ends_b, sib_ends, sib)
    here(2)
    stage(2)

    mine = pl.ds(pl.multiple_of(c * HALF, HALF), HALF)
    rate_h = rate_ref[:, mine]

    def decay(tokens):
        return jnp.exp(-rate_h * float(tokens))

    copies.make(sib_id, sib_ends, sib_ends, sib).wait_recv()
    own_end, other_end = ends[:, mine], sib_ends[:, mine].astype(F32)
    first_end = jnp.where(c == 0, own_end, other_end)
    second_end = jnp.where(c == 0, other_end, own_end)
    total = decay(128) * first_end + second_end
    chip_end[...] = total.astype(BF16)

    here(3)
    y_id, z_id = copies.ids(N), copies.ids(N)
    y_held, z_held = copies.send_ids(N), copies.send_ids(N)
    for k in range(1, N):

        @pl.when(y + k < N)
        def _(k=k):
            copies.make(y_id + k, chip_end, y_in.at[k], at(y + k, z, c), y_held + k).start()

    stage(3)
    stage(4)

    col[...] = jnp.zeros_like(col)
    for k in range(1, N):

        @pl.when(y >= k)
        def _(k=k):
            copies.make(y_id + k, y_in.at[k], y_in.at[k], sib).wait_recv()
            col[...] += decay(2048 * (k - 1)) * y_in[k].astype(F32)

    col_b[...] = col[...].astype(BF16)
    colp_b[...] = (total + decay(2048) * col[...]).astype(BF16)
    for k in range(1, N):

        @pl.when(z + k < N)
        def _(k=k):
            copies.make(z_id + k, colp_b, z_in.at[k], at(y, z + k, c), z_held + k).start()

        @pl.when(z + k >= N)
        def _(k=k):
            copies.make(z_id + k, col_b, z_in.at[k], at(y, z + k - N, c), z_held + k).start()

    stage(5)
    stage(6)

    state = decay(256 * 7) * col[...]
    for k in range(1, N):
        copies.make(z_id + k, z_in.at[k], z_in.at[k], sib).wait_recv()
        state = state + decay(256 * (k - 1)) * z_in[k].astype(F32)
    enter_b[...] = state.astype(BF16)
    enter[:, mine] = state
    enter_id = copies.ids(1)
    copies.send(enter_id, enter_b, sib_enter, sib)
    copies.make(enter_id, sib_enter, sib_enter, sib).wait_recv()
    theirs = pl.ds(pl.multiple_of((1 - c) * HALF, HALF), HALF)
    enter[:, theirs] = sib_enter[...].astype(F32)

    @pl.when(c == 1)
    def _():
        enter[...] = dec[4] * enter[...] + sib_ends[...].astype(F32)


    far = (-float(STEPS)) * block.astype(F32)

    def pass2(lane, carry):
        col_at = pl.ds(pl.multiple_of(lane * 128, 128), 128)
        values = [u[i, :, col_at] for i in range(STEPS)]
        skip = row(skip_ref, pl.ds(0, 1), col_at)

        def one_pole(pole, sums):
            fade = row(dec, 0, pl.ds(pole, 1), col_at)
            gain = row(res_ref, pl.ds(pole, 1), col_at)
            reach = jnp.exp(far * row(rate_ref, pl.ds(pole, 1), col_at))
            state = ent[pole, :, col_at] + reach * row(enter, pl.ds(pole, 1), col_at)
            out = []
            for i in range(STEPS):
                state = fade * state + values[i]
                out.append(sums[i] + gain * state)
            return out

        sums = [skip * value for value in values]
        for pole in range(POLES):
            sums = one_pole(pole, sums)
        for i in range(STEPS):
            g[lane, pl.ds(i, BLK, stride=STEPS), :] = m0[i, :, col_at] * sums[i]
        return carry

    lax.fori_loop(0, LANES, pass2, 0)
    for lane in range(LANES):
        gb[:, lane * 128 : (lane + 1) * 128] = g[lane].astype(BF16)

    def near(of, home_at):
        off = lax.rem(of - home_at + N, N)
        return jnp.where(off <= N // 2, jnp.maximum(2 * off - 1, 0), 2 * (N - off))

    z_slots = [near(i, z) for i in range(N)]
    cores = [c, 1 - c]
    units = [off for offsets in OFFSETS for off in offsets]
    rs, rs_held = copies.ids(12), copies.send_ids(12)
    top, low = pl.ds(0, TOK // 2), pl.ds(TOK // 2, TOK // 2)
    next_dev, prev_dev = (s, x_next), (s, x_prev)

    def place(off):
        y_of = ring(y, off)
        return lax.rem(lax.div(y_of, 2) - t + 4, 4), lax.rem(y_of, 2)

    def project(y_slot, n):
        total = None
        for p in range(2):
            rows = []
            for i in range(8 * n, 8 * n + 8):
                at_z, core = z_slots[i // 2], cores[i % 2]
                rows.append(wbuf[0, core, y_slot, at_z] if p == 0 else wbuf[1, core, at_z, y_slot])
            term = lax.dot_general(
                gb[:, p * HALF : (p + 1) * HALF], jnp.concatenate(rows, axis=0),
                (((1,), (1,)), ((), ())), preferred_element_type=F32,
            )
            total = term if total is None else total + term
        return total

    def shipments(off):
        at_unit = units.index(off)
        _, odd = place(off)
        mine_top, mine_low = part.at[at_unit, top], part.at[at_unit, low]
        far_at, near_at = 2 * odd, 4 + 4 * odd
        far = [(far_at, mine_top, diag.at[at_unit], prev_dev), (far_at + 1, mine_low, diag.at[at_unit], next_dev)]
        nxt = [(near_at, mine_top, arrived.at[odd, 0, top], next_dev), (near_at + 1, mine_low, arrived.at[odd, 0, low], next_dev)]
        prv = [(near_at + 2, mine_low, arrived.at[odd, 1, low], prev_dev), (near_at + 3, mine_top, arrived.at[odd, 1, top], prev_dev)]
        return {
            role: [functools.partial(copies.make, rs + k, *rest, rs_held + k) for k, *rest in ships]
            for role, ships in ((2, far), (1, nxt), (3, prv))
        }

    def begin(off):
        at_unit = units.index(off)
        role, odd = place(off)
        y_slot = at_unit
        for n in range(2):
            cols = slice(n * 256, (n + 1) * 256)
            total = project(y_slot, n)
            part[at_unit, :, cols] = total.astype(BF16)

            @pl.when(role == 0)
            def _(total=total, cols=cols):
                own[odd, :, cols] = total

        ships = shipments(off)

        @pl.when(role == 2)
        def _():
            ships[2][0]().start()
            ships[2][1]().start()

        for side in (1, 3):

            @pl.when(role == side)
            def _(side=side):
                ships[side][0]().start()

    def relay(off):
        at_unit = units.index(off)
        role, odd = place(off)
        ships = shipments(off)
        for side, index, rows in ((1, 1, low), (3, 0, top)):

            @pl.when(role == side)
            def _(side=side, index=index, rows=rows):
                copies.make(rs + 2 * odd + index, diag.at[at_unit], diag.at[at_unit], sib).wait_recv()
                total = part[at_unit, rows, :].astype(F32) + diag[at_unit].astype(F32)
                part[at_unit, rows, :] = total.astype(BF16)
                ships[side][1]().start()

    def finish(off):
        role, odd = place(off)
        ships = shipments(off)

        @pl.when(role == 0)
        def _():
            for k, side, rows in ((0, 0, top), (1, 0, low), (2, 1, low), (3, 1, top)):
                ref = arrived.at[odd, side, rows]
                copies.make(rs + 4 + 4 * odd + k, ref, ref, sib).wait_recv()
            total = own[odd] + arrived[odd, 0].astype(F32) + arrived[odd, 1].astype(F32)
            out_ref[:, pl.ds(pl.multiple_of(odd * WIDE, WIDE), WIDE)] = total.astype(BF16)

        for side in (1, 2, 3):

            @pl.when(role == side)
            def _(side=side):
                for copy in ships[side]:
                    copy().wait_send()

    gathered(0)
    begin(0)
    gathered(1)
    begin(1)
    begin(-1)
    stage(7)
    gathered(2)
    begin(2)
    begin(-2)
    relay(0)
    relay(1)
    relay(-1)
    gathered(3)
    begin(3)
    begin(-3)
    stage(8)
    gathered(4)
    begin(4)
    relay(2)
    relay(-2)
    relay(3)
    relay(-3)
    relay(4)
    for off in units:
        finish(off)

    assert (copies.used, copies.held) == (N_RECV, N_SEND)
    for copy in copies.pool.values():
        copy.wait_send()
    for k in range(1, N):

        @pl.when(y + k < N)
        def _(k=k):
            copies.make(y_id + k, chip_end, y_in.at[k], sib, y_held + k).wait_send()

        copies.make(z_id + k, col_b, z_in.at[k], sib, z_held + k).wait_send()


N_RECV, N_SEND = 127, POOL + 28


def per_device(features, short_taps, rates, residues, skip, out_weight):
    vmem, hbm = pl.BlockSpec(memory_space=pltpu.VMEM), pl.BlockSpec(memory_space=pltpu.HBM)
    return pl.pallas_call(
        kernel,
        out_shape=jax.ShapeDtypeStruct((TOK, CH), BF16),
        in_specs=[hbm] * 6,
        out_specs=vmem,
        scratch_shapes=[
            pltpu.VMEM((2, 2, N, N, 32, HALF), BF16),
            pltpu.VMEM((3, TOK, CH), BF16),
            pltpu.VMEM((3, 8, CH), BF16),
            pltpu.VMEM((3, LANES, TOK + 8, 128), F32),
            pltpu.VMEM((STEPS, BLK, CH), F32),
            pltpu.VMEM((STEPS, BLK, CH), F32),
            pltpu.VMEM((3, 3, CH), BF16),
            pltpu.VMEM((POLES, CH), F32),
            pltpu.VMEM((POLES, CH), F32),
            pltpu.VMEM((1, CH), F32),
            pltpu.VMEM((3, 3, CH), F32),
            pltpu.VMEM((5, POLES, CH), F32),
            pltpu.VMEM((POLES, BLK, CH), F32),
            pltpu.VMEM((POLES, CH), F32),
            pltpu.VMEM((POLES, CH), BF16),
            pltpu.VMEM((POLES, CH), BF16),
            pltpu.VMEM((POLES, HALF), BF16),
            pltpu.VMEM((N, POLES, HALF), BF16),
            pltpu.VMEM((POLES, HALF), BF16),
            pltpu.VMEM((POLES, HALF), BF16),
            pltpu.VMEM((N, POLES, HALF), BF16),
            pltpu.VMEM((POLES, HALF), F32),
            pltpu.VMEM((POLES, CH), F32),
            pltpu.VMEM((POLES, HALF), BF16),
            pltpu.VMEM((POLES, HALF), BF16),
            pltpu.VMEM((LANES, TOK, 128), F32),
            pltpu.VMEM((TOK, CH), BF16),
            pltpu.VMEM((2, TOK, WIDE), F32),
            pltpu.VMEM((N, TOK, WIDE), BF16),
            pltpu.VMEM((N, TOK // 2, WIDE), BF16),
            pltpu.VMEM((2, 2, TOK, WIDE), BF16),
            pltpu.SemaphoreType.DMA((N_SEND,)),
            pltpu.SemaphoreType.DMA((N_RECV,)),
            pltpu.SemaphoreType.DMA((7,)),
            pltpu.SemaphoreType.REGULAR((3,)),
        ],
        compiler_params=pltpu.CompilerParams(
            collective_id=0, has_side_effects=True, vmem_limit_bytes=67043328
        ),
        name="hyena",
    )(
        features.transpose(1, 0, 2),
        short_taps,
        rates.T,
        residues.T,
        skip.reshape(1, CH),
        out_weight,
    )


def solution(mesh):
    in_specs = (
        P("seq", None, "tp"),
        P(None, None, "tp"),
        P("tp", None),
        P("tp", None),
        P("tp"),
        P("seq", "tp"),
    )
    out_specs = P("seq", "tp")
    return jax.shard_map(
        per_device, mesh=mesh, in_specs=in_specs, out_specs=out_specs, check_vma=False
    )
```

```python
import functools

import jax
import jax.numpy as jnp
from jax import lax
from jax.experimental import pallas as pl
from jax.experimental.pallas import tpu as pltpu
from jax.sharding import PartitionSpec as P

MESH = pl.DeviceIdType.MESH
F32, BF16 = jnp.float32, jnp.bfloat16
N = 8
TOK, CH, POLES, OUTS = 128, 1024, 16, 4096
BLK, STEPS = 8, 16
LANES = CH // 128
HALF = CH // 2
DIRS = (1, -1)
POOL = 32
GROUPS = ((0, 1), (1, 3), (3, 5), (5, 7), (7, 8))
OFFSETS = ((0,), (1, -1), (2, -2), (3, -3), (4,))
WIDE = 512
SPLIT = 6


class Copies:
    def __init__(self, send_sem, recv_sem):
        self.send_sem, self.recv_sem, self.used, self.held = send_sem, recv_sem, 0, POOL
        self.pool, self.turn = {}, 0

    def ids(self, count):
        self.used += count
        return self.used - count

    def send_ids(self, count):
        self.held += count
        return self.held - count

    def make(self, index, src, dst, device, held=0):
        return pltpu.make_async_remote_copy(
            src_ref=src,
            dst_ref=dst,
            send_sem=self.send_sem.at[held],
            recv_sem=self.recv_sem.at[index],
            device_id=device,
            device_id_type=MESH,
        )

    def send(self, index, src, dst, device):
        held = self.turn % POOL
        self.turn += 1
        if held in self.pool:
            self.pool[held].wait_send()
        self.pool[held] = self.make(index, src, dst, device, held)
        self.pool[held].start()


def kernel(
    feat_hbm, taps_hbm, rate_hbm, res_hbm, skip_hbm, w_hbm, out_ref,
    wbuf, featb, halo, x, u, m0, taps_ref, rate_ref, res_ref, skip_ref, taps, dec,
    ent, ends, ends_b, sib_ends, chip_end, y_in, col_b, colp_b, z_in, col, enter,
    enter_b, sib_enter, g, gb, own, part, diag, arrived, done, pick,
    send_sem, recv_sem, local_sem, here_sem,
):
    s, t = lax.axis_index("seq"), lax.axis_index("tp")
    c, q = lax.rem(s, 2), lax.div(s, 2)
    z, y = lax.rem(q, N), lax.div(q, N)
    copies = Copies(send_sem, recv_sem)

    def at(y_of, z_of, c_of):
        return ((y_of * N + z_of) * 2 + c_of, t)

    def ring(i, by):
        return lax.rem(i + by + N, N)

    sib = at(y, z, 1 - c)
    after, before = lax.rem(s + 1, 2 * N * N), lax.rem(s + 2 * N * N - 1, 2 * N * N)
    x_next, x_prev, x_far = lax.rem(t + 1, 4), lax.rem(t + 3, 4), lax.rem(t + 2, 4)

    loads = []

    def load(src, dst):
        copy = pltpu.make_async_copy(src, dst, local_sem.at[len(loads)])
        copy.start()
        loads.append(copy)

    barrier = pltpu.get_barrier_semaphore()
    far_seq = jnp.where(c == 0, before, after)
    around = [(y_z, by) for y_z in (0, 1) for by in DIRS]
    around = [at(ring(y, by), z, c) if y_z else at(y, ring(z, by), c) for y_z, by in around]
    partners = [sib, (far_seq, t), (s, x_next), (s, x_prev)] + around
    for partner in partners:
        pl.semaphore_signal(barrier, inc=1, device_id=partner, device_id_type=MESH)
    for p in range(2):
        load(w_hbm.at[:, pl.ds(HALF * p, HALF)], wbuf.at[p, 0, 0, 0])
    load(feat_hbm, featb)
    load(rate_hbm, rate_ref)
    load(taps_hbm, taps_ref)
    load(res_hbm, res_ref)
    load(skip_hbm, skip_ref)
    pl.semaphore_wait(barrier, len(partners))

    def here(round_of):
        if round_of:
            pl.semaphore_wait(here_sem.at[round_of - 1], len(around))
        if round_of < 3:
            for partner in around:
                pl.semaphore_signal(
                    here_sem.at[round_of], inc=1, device_id=partner, device_id_type=MESH
                )

    streams = [(p, d) for d in (0, 1) for p in (0, 1)]
    last = len(GROUPS) - 1

    def carried(d, k):
        return range(last + 1) if k < 3 else (range(3) if d == 0 else range(3, last + 1))

    ring1 = {st: copies.ids(4) for st in streams}
    ring2 = {
        (st, k, group): copies.ids(1)
        for st in streams for k in range(4) for group in carried(st[1], k)
    }
    over = [copies.ids(2) for _ in range(6)]

    def slot(d, k):
        return 0 if k == 0 else N - 1 if k == N // 2 else 2 * k - d

    def target(p, d, inner):
        along_z = (p == 0) == inner
        return at(y, ring(z, DIRS[d]), c) if along_z else at(ring(y, DIRS[d]), z, c)

    def send1(p, d, k):
        src, dst = wbuf.at[p, 0, 0, slot(d, k)], wbuf.at[p, 0, 0, slot(d, k + 1)]
        copies.send(ring1[p, d] + k, src, dst, target(p, d, True))

    def recv1(p, d, k):
        ref = wbuf.at[p, 0, 0, slot(d, k + 1)]
        copies.make(ring1[p, d] + k, ref, ref, sib).wait_recv()

    def outer(p, d, k, group, core=0):
        low, high = GROUPS[group]
        return wbuf.at[p, core, slot(d, k), low:high]

    def send2(p, d, k, group):
        src, dst = outer(p, d, k, group), outer(p, d, k + 1, group)
        copies.send(ring2[(p, d), k, group], src, dst, target(p, d, False))

    def recv2(p, d, k, group):
        ref = outer(p, d, k + 1, group)
        copies.make(ring2[(p, d), k, group], ref, ref, sib).wait_recv()

    def over_refs(m, core):
        low, high = GROUPS[min(m, last)]
        first, end = ((0, N), (0, SPLIT), (SPLIT, N))[max(m - last + 1, 0)]
        return wbuf.at[0, core, low:high, first:end], wbuf.at[1, core, first:end, low:high]

    def stage(n):
        if 1 <= n <= 4:
            for p, d in streams:
                if n < 4 or d == 1:
                    recv1(p, d, n - 1)
                if n < 3 or (n == 3 and d == 1):
                    send1(p, d, n)
        if n == 0:
            for p, d in streams:
                send1(p, d, 0)
        if n <= last:
            for p, d in streams:
                send2(p, d, 0, n)
        for k in range(4):
            group = n - 1 - k
            if not 0 <= group <= last:
                continue
            for p, d in streams:
                if group not in carried(d, k):
                    continue
                recv2(p, d, k, group)
                if k < 3 and group in carried(d, k + 1):
                    send2(p, d, k + 1, group)
        for m in {4: (0,), 5: (1,), 6: (2,), 7: (3, 4), 8: (5,)}.get(n, ()):
            for p in (0, 1):
                copies.send(over[m] + p, over_refs(m, 0)[p], over_refs(m, 1)[p], sib)

    def gathered(m):
        for p in (0, 1):
            ref = over_refs(m, 1)[p]
            copies.make(over[m] + p, ref, ref, sib).wait_recv()

    halo_id = copies.ids(1)
    copies.send(halo_id, feat_hbm.at[:, pl.ds(TOK - 8, 8), :], halo, (after, t))
    here(0)
    for copy in loads[:2]:
        copy.wait()
    stage(0)

    for copy in loads[2:]:
        copy.wait()
    taps[...] = taps_ref[...].astype(F32)
    rate = rate_ref[...]
    for k, span in enumerate((1, 16, 32, 64, 128)):
        dec[k] = jnp.exp(-rate * float(span))
    for group in range(3):
        for lane in range(LANES):
            cut = slice(lane * 128, (lane + 1) * 128)
            x[group, lane, pl.ds(8, TOK), :] = featb[group, :, cut].astype(F32)
    stage(1)
    here(1)
    copies.make(halo_id, halo, halo, sib).wait_recv()
    for group in range(3):
        for lane in range(LANES):
            cut = slice(lane * 128, (lane + 1) * 128)
            edge = jnp.where(s > 0, halo[group, :, cut].astype(F32), 0.0)
            x[group, lane, pl.ds(0, 8), :] = edge

    def row(ref, *index):
        return jnp.broadcast_to(ref[index], (BLK, 128))

    def mix(lane, carry):
        col_at = pl.ds(pl.multiple_of(lane * 128, 128), 128)

        def mixed(group):
            w = [row(taps, group, pl.ds(k, 1), col_at) for k in range(3)]
            v = [x[group, lane, pl.ds(6 + i, BLK, stride=STEPS), :] for i in range(STEPS + 2)]
            return [w[0] * v[i + 2] + w[1] * v[i + 1] + w[2] * v[i] for i in range(STEPS)]

        one, two = mixed(1), mixed(2)
        for i in range(STEPS):
            u[i, :, col_at] = one[i] * two[i]
        for i, value in enumerate(mixed(0)):
            m0[i, :, col_at] = value
        return carry

    lax.fori_loop(0, LANES, mix, 0)

    block = lax.broadcasted_iota(jnp.int32, (BLK, 128), 0)

    def shifted(value, by):
        return jnp.where(block >= by, pltpu.roll(value, by, axis=0), 0.0)

    def pass1(lane, carry):
        col_at = pl.ds(pl.multiple_of(lane * 128, 128), 128)
        values = [u[i, :, col_at] for i in range(STEPS)]
        for pole in range(POLES):
            fade = row(dec, 0, pl.ds(pole, 1), col_at)
            state = values[0]
            for i in range(1, STEPS):
                state = fade * state + values[i]
            for k, by in ((1, 1), (2, 2), (3, 4)):
                state = state + row(dec, k, pl.ds(pole, 1), col_at) * shifted(state, by)
            ent[pole, :, col_at] = shifted(state, 1)
            ends[pl.ds(pole, 1), col_at] = state[BLK - 1 :, :]
        return carry

    lax.fori_loop(0, LANES, pass1, 0)
    ends_b[...] = ends[...].astype(BF16)
    sib_id = copies.ids(1)
    copies.send(sib_id, ends_b, sib_ends, sib)
    here(2)
    stage(2)

    def choose(n, carry):
        rows = pl.ds(pl.multiple_of(n * 128, 128), 128)
        from_at = lax.broadcasted_iota(jnp.int32, (128, WIDE), 0) + n * 128
        to_at = lax.broadcasted_iota(jnp.int32, (128, WIDE), 1)
        off = ((to_at >> 6) - z + N) & (N - 1)
        at_slot = jnp.where(off <= N // 2, jnp.maximum(2 * off - 1, 0), 2 * (N - off))
        pick[rows, :] = (from_at == at_slot * 64 + (to_at & 63)).astype(F32).astype(BF16)
        return carry

    lax.fori_loop(0, WIDE // 128, choose, 0)

    mine = pl.ds(pl.multiple_of(c * HALF, HALF), HALF)
    rate_h = rate_ref[:, mine]

    def decay(tokens):
        return jnp.exp(-rate_h * float(tokens))

    copies.make(sib_id, sib_ends, sib_ends, sib).wait_recv()
    own_end, other_end = ends[:, mine], sib_ends[:, mine].astype(F32)
    first_end = jnp.where(c == 0, own_end, other_end)
    second_end = jnp.where(c == 0, other_end, own_end)
    total = decay(128) * first_end + second_end
    chip_end[...] = total.astype(BF16)

    here(3)
    y_id, z_id = copies.ids(N), copies.ids(N)
    y_held, z_held = copies.send_ids(N), copies.send_ids(N)
    for k in range(1, N):

        @pl.when(y + k < N)
        def _(k=k):
            copies.make(y_id + k, chip_end, y_in.at[k], at(y + k, z, c), y_held + k).start()

    stage(3)
    stage(4)

    col[...] = jnp.zeros_like(col)
    for k in range(1, N):

        @pl.when(y >= k)
        def _(k=k):
            copies.make(y_id + k, y_in.at[k], y_in.at[k], sib).wait_recv()
            col[...] += decay(2048 * (k - 1)) * y_in[k].astype(F32)

    col_b[...] = col[...].astype(BF16)
    colp_b[...] = (total + decay(2048) * col[...]).astype(BF16)
    for k in range(1, N):

        @pl.when(z + k < N)
        def _(k=k):
            copies.make(z_id + k, colp_b, z_in.at[k], at(y, z + k, c), z_held + k).start()

        @pl.when(z + k >= N)
        def _(k=k):
            copies.make(z_id + k, col_b, z_in.at[k], at(y, z + k - N, c), z_held + k).start()

    stage(5)

    state = decay(256 * 7) * col[...]
    for k in range(1, N):
        copies.make(z_id + k, z_in.at[k], z_in.at[k], sib).wait_recv()
        state = state + decay(256 * (k - 1)) * z_in[k].astype(F32)
    enter_b[...] = state.astype(BF16)
    enter[:, mine] = state
    enter_id = copies.ids(1)
    copies.send(enter_id, enter_b, sib_enter, sib)
    stage(6)
    copies.make(enter_id, sib_enter, sib_enter, sib).wait_recv()
    theirs = pl.ds(pl.multiple_of((1 - c) * HALF, HALF), HALF)
    enter[:, theirs] = sib_enter[...].astype(F32)

    @pl.when(c == 1)
    def _():
        enter[...] = dec[4] * enter[...] + sib_ends[...].astype(F32)


    far = (-float(STEPS)) * block.astype(F32)

    def pass2(lane, carry):
        col_at = pl.ds(pl.multiple_of(lane * 128, 128), 128)
        values = [u[i, :, col_at] for i in range(STEPS)]
        skip = row(skip_ref, pl.ds(0, 1), col_at)

        def one_pole(pole, sums):
            fade = row(dec, 0, pl.ds(pole, 1), col_at)
            gain = row(res_ref, pl.ds(pole, 1), col_at)
            reach = jnp.exp(far * row(rate_ref, pl.ds(pole, 1), col_at))
            state = ent[pole, :, col_at] + reach * row(enter, pl.ds(pole, 1), col_at)
            out = []
            for i in range(STEPS):
                state = fade * state + values[i]
                out.append(sums[i] + gain * state)
            return out

        sums = [skip * value for value in values]
        for pole in range(POLES):
            sums = one_pole(pole, sums)
        for i in range(STEPS):
            g[lane, pl.ds(i, BLK, stride=STEPS), :] = m0[i, :, col_at] * sums[i]
        return carry

    lax.fori_loop(0, LANES, pass2, 0)
    for lane in range(LANES):
        gb[:, lane * 128 : (lane + 1) * 128] = g[lane].astype(BF16)

    cores = [c, 1 - c]
    units = [(off, 0, N) for offsets in OFFSETS[:4] for off in offsets]
    units += [(4, 0, SPLIT), (4, SPLIT, N)]
    rs = {later: (copies.ids(12), copies.send_ids(12)) for later in (False, True)}
    top, low = pl.ds(0, TOK // 2), pl.ds(TOK // 2, TOK // 2)
    next_dev, prev_dev = (s, x_next), (s, x_prev)

    def place(off):
        y_of = ring(y, off)
        return lax.rem(lax.div(y_of, 2) - t + 4, 4), lax.rem(y_of, 2)

    def project(y_slot, first, end):
        total = None
        for p in range(2):
            rows = []
            for at_z in range(first, end):
                for core in cores:
                    rows.append(wbuf[0, core, y_slot, at_z] if p == 0 else wbuf[1, core, at_z, y_slot])
            term = lax.dot_general(
                gb[:, p * HALF : (p + 1) * HALF], jnp.concatenate(rows, axis=0),
                (((1,), (1,)), ((), ())), preferred_element_type=F32,
            )
            total = term if total is None else total + term
        return total

    def shipments(unit):
        at_unit, (off, first, end) = min(unit, N - 1), units[unit]
        _, odd = place(off)
        ids, held = rs[first > 0]
        cols = pl.ds(64 * first, 64 * (end - first))
        mine_top, mine_low = part.at[at_unit, top, cols], part.at[at_unit, low, cols]
        far_at, near_at = 2 * odd, 4 + 4 * odd
        far = [(far_at, mine_top, diag.at[at_unit, :, cols], prev_dev), (far_at + 1, mine_low, diag.at[at_unit, :, cols], next_dev)]
        nxt = [(near_at, mine_top, arrived.at[odd, 0, top, cols], next_dev), (near_at + 1, mine_low, arrived.at[odd, 0, low, cols], next_dev)]
        prv = [(near_at + 2, mine_low, arrived.at[odd, 1, low, cols], prev_dev), (near_at + 3, mine_top, arrived.at[odd, 1, top, cols], prev_dev)]
        return {
            role: [functools.partial(copies.make, ids + k, *rest, held + k) for k, *rest in ships]
            for role, ships in ((2, far), (1, nxt), (3, prv))
        }

    def begin(at):
        at_unit, (off, first, end) = min(at, N - 1), units[at]
        role, odd = place(off)
        for start in range(first, end, 4):
            stop = min(start + 4, end)
            cols = slice(start * 64, stop * 64)
            total = project(at_unit, start, stop)
            part[at_unit, :, cols] = total.astype(BF16)

            @pl.when(role == 0)
            def _(total=total, cols=cols):
                own[odd, :, cols] = total

        ships = shipments(at)

        @pl.when(role == 2)
        def _():
            ships[2][0]().start()
            ships[2][1]().start()

        for side in (1, 3):

            @pl.when(role == side)
            def _(side=side):
                ships[side][0]().start()

    def relay(at):
        at_unit, (off, first, end) = min(at, N - 1), units[at]
        role, odd = place(off)
        ships = shipments(at)
        cols = slice(64 * first, 64 * end)
        for side, index, rows in ((1, 1, low), (3, 0, top)):

            @pl.when(role == side)
            def _(side=side, index=index, rows=rows):
                ref = diag.at[at_unit, :, cols]
                copies.make(rs[first > 0][0] + 2 * odd + index, ref, ref, sib).wait_recv()
                total = part[at_unit, rows, cols].astype(F32) + ref[...].astype(F32)
                part[at_unit, rows, cols] = total.astype(BF16)
                ships[side][1]().start()

    def finish(at):
        off, first, end = units[at]
        role, odd = place(off)
        ships = shipments(at)
        cols = slice(64 * first, 64 * end)

        @pl.when(role == 0)
        def _():
            for k, side, rows in ((0, 0, top), (1, 0, low), (2, 1, low), (3, 1, top)):
                ref = arrived.at[odd, side, rows, cols]
                copies.make(rs[first > 0][0] + 4 + 4 * odd + k, ref, ref, sib).wait_recv()
            total = own[odd, :, cols] + arrived[odd, 0, :, cols].astype(F32)
            total = total + arrived[odd, 1, :, cols].astype(F32)
            done[odd, :, cols] = total.astype(BF16)

        for side in (1, 2, 3):

            @pl.when(role == side)
            def _(side=side):
                for copy in ships[side]:
                    copy().wait_send()

    gathered(0)
    begin(0)
    gathered(1)
    begin(1)
    begin(2)
    stage(7)
    gathered(2)
    begin(3)
    begin(4)
    gathered(3)
    begin(5)
    begin(6)
    gathered(4)
    begin(7)
    stage(8)
    relay(0)
    relay(1)
    relay(2)
    gathered(5)
    begin(8)
    relay(3)
    relay(4)
    relay(5)
    relay(6)
    relay(7)
    relay(8)
    for at in range(len(units)):
        finish(at)
    for odd in (0, 1):
        cols = lax.dot_general(
            done[odd], pick[...], (((1,), (0,)), ((), ())), preferred_element_type=F32
        )
        out_ref[:, odd * WIDE : (odd + 1) * WIDE] = cols.astype(BF16)

    assert (copies.used, copies.held) == (N_RECV, N_SEND)
    for copy in copies.pool.values():
        copy.wait_send()
    for k in range(1, N):

        @pl.when(y + k < N)
        def _(k=k):
            copies.make(y_id + k, chip_end, y_in.at[k], sib, y_held + k).wait_send()

        copies.make(z_id + k, col_b, z_in.at[k], sib, z_held + k).wait_send()


N_RECV, N_SEND = 141, POOL + 40


def per_device(features, short_taps, rates, residues, skip, out_weight):
    vmem, hbm = pl.BlockSpec(memory_space=pltpu.VMEM), pl.BlockSpec(memory_space=pltpu.HBM)
    return pl.pallas_call(
        kernel,
        out_shape=jax.ShapeDtypeStruct((TOK, CH), BF16),
        in_specs=[hbm] * 6,
        out_specs=vmem,
        scratch_shapes=[
            pltpu.VMEM((2, 2, N, N, 32, HALF), BF16),
            pltpu.VMEM((3, TOK, CH), BF16),
            pltpu.VMEM((3, 8, CH), BF16),
            pltpu.VMEM((3, LANES, TOK + 8, 128), F32),
            pltpu.VMEM((STEPS, BLK, CH), F32),
            pltpu.VMEM((STEPS, BLK, CH), F32),
            pltpu.VMEM((3, 3, CH), BF16),
            pltpu.VMEM((POLES, CH), F32),
            pltpu.VMEM((POLES, CH), F32),
            pltpu.VMEM((1, CH), F32),
            pltpu.VMEM((3, 3, CH), F32),
            pltpu.VMEM((5, POLES, CH), F32),
            pltpu.VMEM((POLES, BLK, CH), F32),
            pltpu.VMEM((POLES, CH), F32),
            pltpu.VMEM((POLES, CH), BF16),
            pltpu.VMEM((POLES, CH), BF16),
            pltpu.VMEM((POLES, HALF), BF16),
            pltpu.VMEM((N, POLES, HALF), BF16),
            pltpu.VMEM((POLES, HALF), BF16),
            pltpu.VMEM((POLES, HALF), BF16),
            pltpu.VMEM((N, POLES, HALF), BF16),
            pltpu.VMEM((POLES, HALF), F32),
            pltpu.VMEM((POLES, CH), F32),
            pltpu.VMEM((POLES, HALF), BF16),
            pltpu.VMEM((POLES, HALF), BF16),
            pltpu.VMEM((LANES, TOK, 128), F32),
            pltpu.VMEM((TOK, CH), BF16),
            pltpu.VMEM((2, TOK, WIDE), F32),
            pltpu.VMEM((N, TOK, WIDE), BF16),
            pltpu.VMEM((N, TOK // 2, WIDE), BF16),
            pltpu.VMEM((2, 2, TOK, WIDE), BF16),
            pltpu.VMEM((2, TOK, WIDE), BF16),
            pltpu.VMEM((WIDE, WIDE), BF16),
            pltpu.SemaphoreType.DMA((N_SEND,)),
            pltpu.SemaphoreType.DMA((N_RECV,)),
            pltpu.SemaphoreType.DMA((7,)),
            pltpu.SemaphoreType.REGULAR((3,)),
        ],
        compiler_params=pltpu.CompilerParams(
            collective_id=0, has_side_effects=True, vmem_limit_bytes=67043328
        ),
        name="hyena",
    )(
        features.transpose(1, 0, 2),
        short_taps,
        rates.T,
        residues.T,
        skip.reshape(1, CH),
        out_weight,
    )


def solution(mesh):
    in_specs = (
        P("seq", None, "tp"),
        P(None, None, "tp"),
        P("tp", None),
        P("tp", None),
        P("tp"),
        P("seq", "tp"),
    )
    out_specs = P("seq", "tp")
    return jax.shard_map(
        per_device, mesh=mesh, in_specs=in_specs, out_specs=out_specs, check_vma=False
    )
```

```python
import functools

import jax
import jax.numpy as jnp
from jax import lax
from jax.experimental import pallas as pl
from jax.experimental.pallas import tpu as pltpu
from jax.sharding import PartitionSpec as P

MESH = pl.DeviceIdType.MESH
F32, BF16 = jnp.float32, jnp.bfloat16
N = 8
TOK, CH, POLES, OUTS = 128, 1024, 16, 4096
BLK, STEPS = 8, 16
LANES = CH // 128
HALF = CH // 2
DIRS = (1, -1)
POOL = 24
GROUPS = ((0, 1), (1, 3), (3, 5), (5, 7), (7, 8))
OFFSETS = ((0,), (1, -1), (2, -2), (3, -3), (4,))
WIDE = 512
SPLIT = 6


class Copies:
    def __init__(self, send_sem, recv_sem):
        self.send_sem, self.recv_sem, self.used, self.held = send_sem, recv_sem, 0, POOL
        self.pool, self.turn = {}, 0

    def ids(self, count):
        self.used += count
        return self.used - count

    def send_ids(self, count):
        self.held += count
        return self.held - count

    def make(self, index, src, dst, device, held=0):
        return pltpu.make_async_remote_copy(
            src_ref=src,
            dst_ref=dst,
            send_sem=self.send_sem.at[held],
            recv_sem=self.recv_sem.at[index],
            device_id=device,
            device_id_type=MESH,
        )

    def send(self, index, src, dst, device):
        held = self.turn % POOL
        self.turn += 1
        if held in self.pool:
            self.pool[held].wait_send()
        self.pool[held] = self.make(index, src, dst, device, held)
        self.pool[held].start()


def kernel(
    feat_hbm, taps_hbm, rate_hbm, res_hbm, skip_hbm, w_hbm, out_ref,
    wbuf, featb, halo, x, u, m0, taps_ref, rate_ref, res_ref, skip_ref, taps, dec,
    ent, ends, ends_b, sib_ends, chip_end, y_in, col_b, colp_b, z_in, col, enter,
    enter_b, sib_enter, g, gb, own, part, diag, arrived, done, pick,
    send_sem, recv_sem, local_sem, here_sem,
):
    s, t = lax.axis_index("seq"), lax.axis_index("tp")
    c, q = lax.rem(s, 2), lax.div(s, 2)
    z, y = lax.rem(q, N), lax.div(q, N)
    copies = Copies(send_sem, recv_sem)

    def at(y_of, z_of, c_of):
        return ((y_of * N + z_of) * 2 + c_of, t)

    def ring(i, by):
        return lax.rem(i + by + N, N)

    sib = at(y, z, 1 - c)
    after, before = lax.rem(s + 1, 2 * N * N), lax.rem(s + 2 * N * N - 1, 2 * N * N)
    x_next, x_prev, x_far = lax.rem(t + 1, 4), lax.rem(t + 3, 4), lax.rem(t + 2, 4)

    loads = []

    def load(src, dst):
        copy = pltpu.make_async_copy(src, dst, local_sem.at[len(loads)])
        copy.start()
        loads.append(copy)

    barrier = pltpu.get_barrier_semaphore()
    far_seq = jnp.where(c == 0, before, after)
    around = [(y_z, by) for y_z in (0, 1) for by in DIRS]
    around = [at(ring(y, by), z, c) if y_z else at(y, ring(z, by), c) for y_z, by in around]
    partners = [sib, (far_seq, t), (s, x_next), (s, x_prev)] + around
    for partner in partners:
        pl.semaphore_signal(barrier, inc=1, device_id=partner, device_id_type=MESH)
    for p in range(2):
        load(w_hbm.at[:, pl.ds(HALF * p, HALF)], wbuf.at[p, 0, 0, 0])
    load(feat_hbm, featb)
    load(rate_hbm, rate_ref)
    load(taps_hbm, taps_ref)
    load(res_hbm, res_ref)
    load(skip_hbm, skip_ref)
    pl.semaphore_wait(barrier, len(partners))

    def here(round_of):
        if round_of:
            pl.semaphore_wait(here_sem.at[round_of - 1], len(around))
        if round_of < 3:
            for partner in around:
                pl.semaphore_signal(
                    here_sem.at[round_of], inc=1, device_id=partner, device_id_type=MESH
                )

    streams = [(p, d) for d in (0, 1) for p in (0, 1)]
    last = len(GROUPS) - 1

    def carried(d, k):
        return range(last + 1) if k < 3 else (range(3) if d == 0 else range(3, last + 1))

    ring1 = {st: copies.ids(4) for st in streams}
    ring2 = {
        (st, k, group): copies.ids(1)
        for st in streams for k in range(4) for group in carried(st[1], k)
    }
    over = [copies.ids(2) for _ in range(6)]

    def slot(d, k):
        return 0 if k == 0 else N - 1 if k == N // 2 else 2 * k - d

    def target(p, d, inner):
        along_z = (p == 0) == inner
        return at(y, ring(z, DIRS[d]), c) if along_z else at(ring(y, DIRS[d]), z, c)

    def send1(p, d, k):
        src, dst = wbuf.at[p, 0, 0, slot(d, k)], wbuf.at[p, 0, 0, slot(d, k + 1)]
        copies.send(ring1[p, d] + k, src, dst, target(p, d, True))

    def recv1(p, d, k):
        ref = wbuf.at[p, 0, 0, slot(d, k + 1)]
        copies.make(ring1[p, d] + k, ref, ref, sib).wait_recv()

    def outer(p, d, k, group, core=0):
        low, high = GROUPS[group]
        return wbuf.at[p, core, slot(d, k), low:high]

    def send2(p, d, k, group):
        src, dst = outer(p, d, k, group), outer(p, d, k + 1, group)
        copies.send(ring2[(p, d), k, group], src, dst, target(p, d, False))

    def recv2(p, d, k, group):
        ref = outer(p, d, k + 1, group)
        copies.make(ring2[(p, d), k, group], ref, ref, sib).wait_recv()

    def over_refs(m, core):
        low, high = GROUPS[min(m, last)]
        first, end = ((0, N), (0, SPLIT), (SPLIT, N))[max(m - last + 1, 0)]
        return wbuf.at[0, core, low:high, first:end], wbuf.at[1, core, first:end, low:high]

    def stage(n):
        if 1 <= n <= 4:
            for p, d in streams:
                if n < 4 or d == 1:
                    recv1(p, d, n - 1)
                if n < 3 or (n == 3 and d == 1):
                    send1(p, d, n)
        if n == 0:
            for p, d in streams:
                send1(p, d, 0)
        if n <= last:
            for p, d in streams:
                send2(p, d, 0, n)
        for k in range(4):
            group = n - 1 - k
            if not 0 <= group <= last:
                continue
            for p, d in streams:
                if group not in carried(d, k):
                    continue
                recv2(p, d, k, group)
                if k < 3 and group in carried(d, k + 1):
                    send2(p, d, k + 1, group)
        for m in {4: (0,), 5: (1,), 6: (2,), 7: (3, 4), 8: (5,)}.get(n, ()):
            for p in (0, 1):
                copies.send(over[m] + p, over_refs(m, 0)[p], over_refs(m, 1)[p], sib)

    def gathered(m):
        for p in (0, 1):
            ref = over_refs(m, 1)[p]
            copies.make(over[m] + p, ref, ref, sib).wait_recv()

    halo_id = copies.ids(1)
    copies.send(halo_id, feat_hbm.at[:, pl.ds(TOK - 8, 8), :], halo, (after, t))
    here(0)
    for copy in loads[:2]:
        copy.wait()
    stage(0)

    for copy in loads[2:]:
        copy.wait()
    taps[...] = taps_ref[...].astype(F32)
    rate = rate_ref[...]
    for k, span in enumerate((1, 16, 32, 64, 128)):
        dec[k] = jnp.exp(-rate * float(span))
    for group in range(3):
        for lane in range(LANES):
            cut = slice(lane * 128, (lane + 1) * 128)
            x[group, lane, pl.ds(8, TOK), :] = featb[group, :, cut].astype(F32)
    stage(1)
    here(1)
    copies.make(halo_id, halo, halo, sib).wait_recv()
    for group in range(3):
        for lane in range(LANES):
            cut = slice(lane * 128, (lane + 1) * 128)
            edge = jnp.where(s > 0, halo[group, :, cut].astype(F32), 0.0)
            x[group, lane, pl.ds(0, 8), :] = edge

    def row(ref, *index):
        return jnp.broadcast_to(ref[index], (BLK, 128))

    def mix(lane, carry):
        col_at = pl.ds(pl.multiple_of(lane * 128, 128), 128)

        def mixed(group):
            w = [row(taps, group, pl.ds(k, 1), col_at) for k in range(3)]
            v = [x[group, lane, pl.ds(6 + i, BLK, stride=STEPS), :] for i in range(STEPS + 2)]
            return [w[0] * v[i + 2] + w[1] * v[i + 1] + w[2] * v[i] for i in range(STEPS)]

        one, two = mixed(1), mixed(2)
        for i in range(STEPS):
            u[i, :, col_at] = one[i] * two[i]
        for i, value in enumerate(mixed(0)):
            m0[i, :, col_at] = value
        return carry

    lax.fori_loop(0, LANES, mix, 0)

    block = lax.broadcasted_iota(jnp.int32, (BLK, 128), 0)

    def shifted(value, by):
        return jnp.where(block >= by, pltpu.roll(value, by, axis=0), 0.0)

    def pass1(lane, carry):
        col_at = pl.ds(pl.multiple_of(lane * 128, 128), 128)
        values = [u[i, :, col_at] for i in range(STEPS)]
        for pole in range(POLES):
            fade = row(dec, 0, pl.ds(pole, 1), col_at)
            state = values[0]
            for i in range(1, STEPS):
                state = fade * state + values[i]
            for k, by in ((1, 1), (2, 2), (3, 4)):
                state = state + row(dec, k, pl.ds(pole, 1), col_at) * shifted(state, by)
            ent[pole, :, col_at] = shifted(state, 1)
            ends[pl.ds(pole, 1), col_at] = state[BLK - 1 :, :]
        return carry

    lax.fori_loop(0, LANES, pass1, 0)
    ends_b[...] = ends[...].astype(BF16)
    sib_id = copies.ids(1)
    copies.send(sib_id, ends_b, sib_ends, sib)
    here(2)
    stage(2)

    def choose(n, carry):
        rows = pl.ds(pl.multiple_of(n * 128, 128), 128)
        from_at = lax.broadcasted_iota(jnp.int32, (128, WIDE), 0) + n * 128
        to_at = lax.broadcasted_iota(jnp.int32, (128, WIDE), 1)
        off = ((to_at >> 6) - z + N) & (N - 1)
        at_slot = jnp.where(off <= N // 2, jnp.maximum(2 * off - 1, 0), 2 * (N - off))
        pick[rows, :] = (from_at == at_slot * 64 + (to_at & 63)).astype(F32).astype(BF16)
        return carry

    lax.fori_loop(0, WIDE // 128, choose, 0)

    mine = pl.ds(pl.multiple_of(c * HALF, HALF), HALF)
    rate_h = rate_ref[:, mine]

    def decay(tokens):
        return jnp.exp(-rate_h * float(tokens))

    copies.make(sib_id, sib_ends, sib_ends, sib).wait_recv()
    own_end, other_end = ends[:, mine], sib_ends[:, mine].astype(F32)
    first_end = jnp.where(c == 0, own_end, other_end)
    second_end = jnp.where(c == 0, other_end, own_end)
    total = decay(128) * first_end + second_end
    chip_end[...] = total.astype(BF16)

    here(3)
    y_id, z_id = copies.ids(N), copies.ids(N)
    y_held, z_held = copies.send_ids(N), copies.send_ids(N)
    for k in range(1, N):

        @pl.when(y + k < N)
        def _(k=k):
            copies.make(y_id + k, chip_end, y_in.at[k], at(y + k, z, c), y_held + k).start()

    stage(3)
    stage(4)

    col[...] = jnp.zeros_like(col)
    for k in range(1, N):

        @pl.when(y >= k)
        def _(k=k):
            copies.make(y_id + k, y_in.at[k], y_in.at[k], sib).wait_recv()
            col[...] += decay(2048 * (k - 1)) * y_in[k].astype(F32)

    col_b[...] = col[...].astype(BF16)
    colp_b[...] = (total + decay(2048) * col[...]).astype(BF16)
    for k in range(1, N):

        @pl.when(z + k < N)
        def _(k=k):
            copies.make(z_id + k, colp_b, z_in.at[k], at(y, z + k, c), z_held + k).start()

        @pl.when(z + k >= N)
        def _(k=k):
            copies.make(z_id + k, col_b, z_in.at[k], at(y, z + k - N, c), z_held + k).start()

    stage(5)

    state = decay(256 * 7) * col[...]
    for k in range(1, N):
        copies.make(z_id + k, z_in.at[k], z_in.at[k], sib).wait_recv()
        state = state + decay(256 * (k - 1)) * z_in[k].astype(F32)
    enter_b[...] = state.astype(BF16)
    enter[:, mine] = state
    enter_id = copies.ids(1)
    copies.send(enter_id, enter_b, sib_enter, sib)
    stage(6)
    copies.make(enter_id, sib_enter, sib_enter, sib).wait_recv()
    theirs = pl.ds(pl.multiple_of((1 - c) * HALF, HALF), HALF)
    enter[:, theirs] = sib_enter[...].astype(F32)

    @pl.when(c == 1)
    def _():
        enter[...] = dec[4] * enter[...] + sib_ends[...].astype(F32)


    far = (-float(STEPS)) * block.astype(F32)

    def pass2(lane, carry):
        col_at = pl.ds(pl.multiple_of(lane * 128, 128), 128)
        values = [u[i, :, col_at] for i in range(STEPS)]
        skip = row(skip_ref, pl.ds(0, 1), col_at)

        def one_pole(pole, sums):
            fade = row(dec, 0, pl.ds(pole, 1), col_at)
            gain = row(res_ref, pl.ds(pole, 1), col_at)
            reach = jnp.exp(far * row(rate_ref, pl.ds(pole, 1), col_at))
            state = ent[pole, :, col_at] + reach * row(enter, pl.ds(pole, 1), col_at)
            out = []
            for i in range(STEPS):
                state = fade * state + values[i]
                out.append(sums[i] + gain * state)
            return out

        sums = [skip * value for value in values]
        for pole in range(POLES):
            sums = one_pole(pole, sums)
        for i in range(STEPS):
            g[lane, pl.ds(i, BLK, stride=STEPS), :] = m0[i, :, col_at] * sums[i]
        return carry

    lax.fori_loop(0, LANES, pass2, 0)
    for lane in range(LANES):
        gb[:, lane * 128 : (lane + 1) * 128] = g[lane, pl.ds(0, TOK), :].astype(BF16)

    cores = [c, 1 - c]
    units = [(off, 0, N) for offsets in OFFSETS[:4] for off in offsets]
    units += [(4, 0, SPLIT), (4, SPLIT, N)]
    rs = {later: (copies.ids(12), copies.send_ids(12)) for later in (False, True)}
    top, low = pl.ds(0, TOK // 2), pl.ds(TOK // 2, TOK // 2)
    next_dev, prev_dev = (s, x_next), (s, x_prev)

    def place(off):
        y_of = ring(y, off)
        return lax.rem(lax.div(y_of, 2) - t + 4, 4), lax.rem(y_of, 2)

    def project(y_slot, first, end):
        total = None
        for p in range(2):
            rows = []
            for at_z in range(first, end):
                for core in cores:
                    rows.append(wbuf[0, core, y_slot, at_z] if p == 0 else wbuf[1, core, at_z, y_slot])
            term = lax.dot_general(
                gb[:, p * HALF : (p + 1) * HALF], jnp.concatenate(rows, axis=0),
                (((1,), (1,)), ((), ())), preferred_element_type=F32,
            )
            total = term if total is None else total + term
        return total

    def shipments(unit):
        at_unit, (off, first, end) = min(unit, N - 1), units[unit]
        _, odd = place(off)
        ids, held = rs[first > 0]
        cols = pl.ds(64 * first, 64 * (end - first))
        mine_top, mine_low = part.at[at_unit, top, cols], part.at[at_unit, low, cols]
        far_at, near_at = 2 * odd, 4 + 4 * odd
        far = [(far_at, mine_top, diag.at[at_unit, :, cols], prev_dev), (far_at + 1, mine_low, diag.at[at_unit, :, cols], next_dev)]
        nxt = [(near_at, mine_top, arrived.at[odd, 0, top, cols], next_dev), (near_at + 1, mine_low, arrived.at[odd, 0, low, cols], next_dev)]
        prv = [(near_at + 2, mine_low, arrived.at[odd, 1, low, cols], prev_dev), (near_at + 3, mine_top, arrived.at[odd, 1, top, cols], prev_dev)]
        return {
            role: [functools.partial(copies.make, ids + k, *rest, held + k) for k, *rest in ships]
            for role, ships in ((2, far), (1, nxt), (3, prv))
        }

    def begin(at):
        at_unit, (off, first, end) = min(at, N - 1), units[at]
        role, odd = place(off)
        for start in range(first, end, 4):
            stop = min(start + 4, end)
            cols = slice(start * 64, stop * 64)
            total = project(at_unit, start, stop)
            part[at_unit, :, cols] = total.astype(BF16)

            @pl.when(role == 0)
            def _(total=total, cols=cols):
                own[odd, :, cols] = total

        ships = shipments(at)

        @pl.when(role == 2)
        def _():
            ships[2][0]().start()
            ships[2][1]().start()

        for side in (1, 3):

            @pl.when(role == side)
            def _(side=side):
                ships[side][0]().start()

    def relay(at):
        at_unit, (off, first, end) = min(at, N - 1), units[at]
        role, odd = place(off)
        ships = shipments(at)
        cols = slice(64 * first, 64 * end)
        for side, index, rows in ((1, 1, low), (3, 0, top)):

            @pl.when(role == side)
            def _(side=side, index=index, rows=rows):
                ref = diag.at[at_unit, :, cols]
                copies.make(rs[first > 0][0] + 2 * odd + index, ref, ref, sib).wait_recv()
                total = part[at_unit, rows, cols].astype(F32) + ref[...].astype(F32)
                part[at_unit, rows, cols] = total.astype(BF16)
                ships[side][1]().start()

    def finish(at):
        off, first, end = units[at]
        role, odd = place(off)
        ships = shipments(at)
        cols = slice(64 * first, 64 * end)

        @pl.when(role == 0)
        def _():
            for k, side, rows in ((0, 0, top), (1, 0, low), (2, 1, low), (3, 1, top)):
                ref = arrived.at[odd, side, rows, cols]
                copies.make(rs[first > 0][0] + 4 + 4 * odd + k, ref, ref, sib).wait_recv()
            total = own[odd, :, cols] + arrived[odd, 0, :, cols].astype(F32)
            total = total + arrived[odd, 1, :, cols].astype(F32)
            done[odd, :, cols] = total.astype(BF16)

        for side in (1, 2, 3):

            @pl.when(role == side)
            def _(side=side):
                for copy in ships[side]:
                    copy().wait_send()

    gathered(0)
    begin(0)
    gathered(1)
    begin(1)
    begin(2)
    stage(7)
    gathered(2)
    begin(3)
    begin(4)
    gathered(3)
    begin(5)
    begin(6)
    gathered(4)
    begin(7)
    stage(8)
    gathered(5)
    begin(8)
    relay(0)
    relay(1)
    relay(2)
    relay(3)
    relay(4)
    relay(5)
    relay(6)
    relay(7)
    relay(8)
    finish(0)
    finish(1)
    finish(2)
    finish(3)
    finish(4)
    finish(5)
    finish(6)
    finish(7)
    finish(8)
    for odd in (0, 1):
        cols = lax.dot_general(
            done[odd], pick[...], (((1,), (0,)), ((), ())), preferred_element_type=F32
        )
        out_ref[:, odd * WIDE : (odd + 1) * WIDE] = cols.astype(BF16)

    assert (copies.used, copies.held) == (N_RECV, N_SEND)
    for copy in copies.pool.values():
        copy.wait_send()
    for k in range(1, N):

        @pl.when(y + k < N)
        def _(k=k):
            copies.make(y_id + k, chip_end, y_in.at[k], sib, y_held + k).wait_send()

        copies.make(z_id + k, col_b, z_in.at[k], sib, z_held + k).wait_send()


N_RECV, N_SEND = 141, POOL + 40


def per_device(features, short_taps, rates, residues, skip, out_weight):
    vmem, hbm = pl.BlockSpec(memory_space=pltpu.VMEM), pl.BlockSpec(memory_space=pltpu.HBM)
    return pl.pallas_call(
        kernel,
        out_shape=jax.ShapeDtypeStruct((TOK, CH), BF16),
        in_specs=[hbm] * 6,
        out_specs=vmem,
        scratch_shapes=[
            pltpu.VMEM((2, 2, N, N, 32, HALF), BF16),
            pltpu.VMEM((3, TOK, CH), BF16),
            pltpu.VMEM((3, 8, CH), BF16),
            pltpu.VMEM((3, LANES, TOK + 24, 128), F32),
            pltpu.VMEM((STEPS, BLK, CH), F32),
            pltpu.VMEM((STEPS, BLK, CH), F32),
            pltpu.VMEM((3, 3, CH), BF16),
            pltpu.VMEM((POLES, CH), F32),
            pltpu.VMEM((POLES, CH), F32),
            pltpu.VMEM((1, CH), F32),
            pltpu.VMEM((3, 3, CH), F32),
            pltpu.VMEM((5, POLES, CH), F32),
            pltpu.VMEM((POLES, BLK, CH), F32),
            pltpu.VMEM((POLES, CH), F32),
            pltpu.VMEM((POLES, CH), BF16),
            pltpu.VMEM((POLES, CH), BF16),
            pltpu.VMEM((POLES, HALF), BF16),
            pltpu.VMEM((N, POLES, HALF), BF16),
            pltpu.VMEM((POLES, HALF), BF16),
            pltpu.VMEM((POLES, HALF), BF16),
            pltpu.VMEM((N, POLES, HALF), BF16),
            pltpu.VMEM((POLES, HALF), F32),
            pltpu.VMEM((POLES, CH), F32),
            pltpu.VMEM((POLES, HALF), BF16),
            pltpu.VMEM((POLES, HALF), BF16),
            pltpu.VMEM((LANES, TOK + STEPS, 128), F32),
            pltpu.VMEM((TOK, CH), BF16),
            pltpu.VMEM((2, TOK, WIDE), F32),
            pltpu.VMEM((N, TOK, WIDE), BF16),
            pltpu.VMEM((N, TOK // 2, WIDE), BF16),
            pltpu.VMEM((2, 2, TOK, WIDE), BF16),
            pltpu.VMEM((2, TOK, WIDE), BF16),
            pltpu.VMEM((WIDE, WIDE), BF16),
            pltpu.SemaphoreType.DMA((N_SEND,)),
            pltpu.SemaphoreType.DMA((N_RECV,)),
            pltpu.SemaphoreType.DMA((7,)),
            pltpu.SemaphoreType.REGULAR((3,)),
        ],
        compiler_params=pltpu.CompilerParams(
            collective_id=0, has_side_effects=True, vmem_limit_bytes=67043328
        ),
        name="hyena",
    )(
        features.transpose(1, 0, 2),
        short_taps,
        rates.T,
        residues.T,
        skip.reshape(1, CH),
        out_weight,
    )


def solution(mesh):
    in_specs = (
        P("seq", None, "tp"),
        P(None, None, "tp"),
        P("tp", None),
        P("tp", None),
        P("tp"),
        P("seq", "tp"),
    )
    out_specs = P("seq", "tp")
    return jax.shard_map(
        per_device, mesh=mesh, in_specs=in_specs, out_specs=out_specs, check_vma=False
    )
```
